32 devices in a mesh: sec: 2 (over y), grp: 4 (over x, core), seq: 4 (over z).
Axes of the slice: x: 2, y: 2, z: 4, core: 2. Of those that a mesh axis runs over, the one named last changes fastest.
Arguments:
- tokens: bfloat16 [8192, 1024], P(('sec', 'grp', 'seq')), may hold values from -6 to 6
- expert_ids: int32 [8192, 1], P(('sec', 'grp', 'seq')), may hold values from 0 to 31; in each aligned block of 256 rows (0 to 255, 256 to 511, ...) at most 16 rows name the same one
- attn_in: bfloat16 [1024, 3072], replicated
- attn_out: bfloat16 [1024, 1024], replicated, may hold values from -0.1875 to 0.1875
- gain_attn: float32 [1024], replicated, may hold values from 0.5 to 1.5
- gain_expert: float32 [1024], replicated, may hold values from 0.5 to 1.5
- router: bfloat16 [1024, 32], replicated, may hold values from -0.1875 to 0.1875
- expert_in: bfloat16 [32, 1024, 2816], P(('sec', 'grp', 'seq')), may hold values from -0.1875 to 0.1875
- expert_out: bfloat16 [32, 2816, 1024], P(('sec', 'grp', 'seq')), may hold values from -0.109375 to 0.109375
Outputs:
- layer_out: bfloat16 [8192, 1024], P(('sec', 'grp', 'seq'))
The draws below stay inside these ranges and needn't reach their ends.
Inputs may be any that keep to these rules, and one draw needn't show every extreme that they name: `expert_ids`: of the 256 tokens of one device at most 16 choose one expert, and on every device some expert is chosen by exactly 16 of them.
All inputs are finite; a program needn't handle non-finite values.
Results may differ from the reference program's by a relative error of at most 0.004.
Values may be sent and summed in bfloat16 or wider, within the bound.
A program may use at most 192 MiB of HBM per device.

```python
import math
import jax
import jax.numpy as jnp
import numpy as np
from jax import lax

D = 1024
HEADS = 16
FF = 2816
TOK_DEV = 256
HEAD_DIM = 64
EXPERTS = 32
MOST = 16
LENGTH = 1024
TOKENS = 8192


def draw_attn_in(key, part):
    values = jax.random.normal(key, (D, 3 * D), jnp.float32) * D ** (-0.5)
    return values.astype(jnp.bfloat16)


def block_scale(key, extent, shards, smallest, largest):
    level = 1.0
    for dim, shards_of in shards:
        heights = jax.random.uniform(jax.random.fold_in(jax.random.fold_in(key, 6), dim), (shards_of,), jnp.float32, smallest / len(shards), largest / len(shards))
        level = level * jnp.repeat(jnp.exp(heights), extent[dim] // shards_of).reshape((-1,) + (1,) * (len(extent) - 1 - dim))
    return level


def deal_out(rng, own, number, rows, number_of, top, reach, slope):
    sequence = jax.random.permutation(rng, number_of)
    packed, usual = shares(number_of, rows * top, reach, slope, True), shares(number_of, rows * top, reach, slope, False)
    places = jnp.arange(number_of)

    def named(sizes, offset_by):
        used = int((sizes > 0).sum())
        fixed = max(1, used // 4)
        shifted = fixed + (places - fixed + offset_by * (used - fixed)) % max(1, number_of - fixed)
        return jnp.zeros((number_of,), jnp.int32).at[sequence[jnp.where(places < fixed, places, shifted)]].set(jnp.asarray(sizes, jnp.int32))

    sizes = jnp.where(number % 4 == 0, named(packed, number // 4), named(usual, number - number // 4 - 1))
    mixed = jax.random.permutation(jax.random.fold_in(own, 3), number_of)
    source_of, taker = mixed[0:number_of // 2 * 2:2], mixed[1:number_of // 2 * 2:2]
    margin = jnp.minimum(sizes[source_of] - 1, reach - sizes[taker]) // 2
    margin = jnp.where((source_of == sequence[0]) | (taker == sequence[0]) | (sizes[taker] == 0), 0, jnp.maximum(margin, 0))
    shifted = jax.random.randint(jax.random.fold_in(own, 4), (number_of // 2,), 0, 1 << 20) % (margin + 1)
    sizes = sizes.at[source_of].add(-shifted).at[taker].add(shifted)
    labels = jnp.searchsorted(jnp.cumsum(sizes), jnp.arange(rows * top), side="right").astype(jnp.int32)
    listing = labels.reshape(top, rows).T
    listing = listing[jax.random.permutation(jax.random.fold_in(own, 1), rows)]
    offset_by = jax.random.randint(jax.random.fold_in(own, 2), (rows, 1), 0, top)
    return jnp.take_along_axis(listing, (jnp.arange(top)[None, :] + offset_by) % top, axis=1)


def shares(amount, total, limit, lean, full):
    portions = [(1 << 20) // math.isqrt(rank ** lean) + 1 for rank in range(1, amount + 1)]
    largest = limit if full else min(limit, max(-(-total // amount), total * portions[0] // sum(portions)))
    least = 1 if total - largest >= amount - 1 else 0
    given, spare = [largest] + [least] * (amount - 1), total - largest - least * (amount - 1)
    while spare > 0:
        movable = [i for i in range(1, amount) if given[i] < largest] or [i for i in range(1, amount) if given[i] < limit]
        whole, remaining = sum([portions[i] for i in movable]), spare
        for i in movable:
            addition = min(limit - given[i], max(1, remaining * portions[i] // whole), spare)
            given[i] = given[i] + addition
            spare = spare - addition
    return np.array(given)


def centred(key, extent, deviation, bound, shards=(), kind=jnp.bfloat16):
    result = deviation * jax.random.normal(key, extent, jnp.float32)
    if shards:
        result = result * block_scale(key, extent, shards, -0.22, 0.18)
    return jnp.clip(result, -bound, bound).astype(kind)


def setup_inputs(seed: int = 0) -> dict:
    splits = jax.random.split(jax.random.key(seed), 10)
    tokens = centred(splits[0], (TOKENS, D), 1.0, 6.0, ((0, 32),))
    expert_ids_keys = jax.random.split(jax.random.fold_in(splits[1], 1), TOKENS // TOK_DEV)
    expert_ids_turns = jax.random.permutation(jax.random.fold_in(splits[1], 3), TOKENS // TOK_DEV)
    expert_ids = jax.vmap(lambda own, number: deal_out(jax.random.fold_in(splits[1], 2), own, number, TOK_DEV, EXPERTS, 1, MOST, 1))(expert_ids_keys, expert_ids_turns).reshape((TOKENS, 1))
    attn_in = draw_attn_in(jax.random.fold_in(splits[9], 71), 0)
    attn_out = centred(splits[3], (D, D), D ** -0.5, 0.1875)
    gain_attn = jnp.clip(1.0 + 0.1 * jax.random.normal(splits[4], (D,), jnp.float32), 0.5, 1.5)
    gain_expert = jnp.clip(1.0 + 0.1 * jax.random.normal(splits[5], (D,), jnp.float32), 0.5, 1.5)
    router = centred(splits[6], (D, EXPERTS), D ** -0.5, 0.1875)
    expert_in = centred(splits[7], (EXPERTS, D, FF), D ** -0.5, 0.1875, ((0, 32),))
    expert_out = centred(splits[8], (EXPERTS, FF, D), FF ** -0.5, 0.109375, ((0, 32),))
    return dict(tokens=tokens, expert_ids=expert_ids, attn_in=attn_in, attn_out=attn_out, gain_attn=gain_attn, gain_expert=gain_expert, router=router, expert_in=expert_in, expert_out=expert_out)


def normalize(values, gain):
    return values * lax.rsqrt(lax.optimization_barrier(jnp.mean(values * values, -1, keepdims=True)) + 1e-06) * gain.astype(jnp.float32)

def head_attention(query, keys, values):
    scores = jnp.dot(query, keys.T, preferred_element_type=jnp.float32) * query.shape[1] ** (-0.5)
    weights = jax.nn.softmax(scores, -1).astype(jnp.bfloat16)
    return jnp.dot(weights, values, preferred_element_type=jnp.float32).astype(jnp.bfloat16)

def reference(tokens, expert_ids, attn_in, attn_out, gain_attn, gain_expert, router, expert_in, expert_out):
    tokens_f32 = tokens.astype(jnp.float32)
    normed = normalize(tokens_f32, gain_attn).astype(jnp.bfloat16)
    projected = jnp.dot(normed, attn_in, preferred_element_type=jnp.float32).astype(jnp.bfloat16)
    seq_count = TOKENS // LENGTH
    head_parts = projected.reshape(seq_count, LENGTH, 3, HEADS, HEAD_DIM).transpose(0, 3, 2, 1, 4)
    head_parts = head_parts.reshape(seq_count * HEADS, 3, LENGTH, HEAD_DIM)
    context = lax.map(lambda head_item: head_attention(head_item[0], head_item[1], head_item[2]), head_parts)
    context = context.reshape(seq_count, HEADS, LENGTH, HEAD_DIM).transpose(0, 2, 1, 3).reshape(TOKENS, D)
    hidden = tokens_f32 + jnp.dot(context, attn_out, preferred_element_type=jnp.float32)
    normed2 = normalize(hidden, gain_expert).astype(jnp.bfloat16)
    picked = expert_ids[:, 0]
    logits = jnp.dot(normed2, router, preferred_element_type=jnp.float32)
    gate_value = jax.nn.sigmoid(jnp.take_along_axis(logits, expert_ids, 1)[:, 0])
    capacity = TOKENS // TOK_DEV * MOST
    padded_rows = jnp.concatenate([normed2, jnp.zeros((1, D), jnp.bfloat16)], 0)

    def one_expert(expert_index):
        slot_rows = jnp.nonzero(picked == expert_index, size=capacity, fill_value=TOKENS)[0].astype(jnp.int32)
        inputs = padded_rows[slot_rows]
        inner_act = jax.nn.relu(jnp.dot(inputs, expert_in[expert_index], preferred_element_type=jnp.float32)).astype(jnp.bfloat16)
        return (slot_rows, jnp.dot(inner_act, expert_out[expert_index], preferred_element_type=jnp.float32).astype(jnp.bfloat16))
    slot_rows, outputs = lax.map(one_expert, jnp.arange(EXPERTS, dtype=jnp.int32))
    combined = jnp.zeros((TOKENS + 1, D), jnp.float32).at[slot_rows.reshape(-1)].add(outputs.reshape(-1, D).astype(jnp.float32))
    combined = combined[:TOKENS]
    return (hidden + gate_value[:, None] * combined).astype(jnp.bfloat16)
```

```python
import functools

import jax
import jax.numpy as jnp
from jax import lax
from jax.experimental import pallas as pl
from jax.experimental.pallas import tpu as pltpu
from jax.sharding import PartitionSpec as P

HEADS = 16
AXES = ("sec", "grp", "seq")
MESH = pl.DeviceIdType.MESH
VMEM_LIMIT = 60 * 1024 * 1024


def normalize(values, gain):
    return values * lax.rsqrt(jnp.mean(values * values, -1, keepdims=True) + 1e-06) * gain


def attention_kernel(
    ranks,
    head_dim,
    tok_ref,
    win_hbm,
    wout_hbm,
    gain_ref,
    gain2_ref,
    hidden_ref,
    normed2_ref,
    shards,
    win,
    wout,
    query2,
    kv,
    acc,
    top,
    total,
    context,
    w_sem,
    right_sem,
    left_sem,
    recv_sem,
):
    rows, width = tok_ref.shape
    pair = 2 * head_dim
    pairs = width // pair
    me = lax.axis_index("seq")
    load_in = pltpu.make_async_copy(win_hbm, win, w_sem.at[0])
    load_out = pltpu.make_async_copy(wout_hbm, wout, w_sem.at[1])
    load_in.start()
    load_out.start()
    has_left, has_right = me > 0, me < ranks - 1
    barrier = pltpu.get_barrier_semaphore()

    @pl.when(has_left)
    def _():
        pl.semaphore_signal(barrier, inc=1, device_id={"seq": me - 1}, device_id_type=MESH)

    @pl.when(has_right)
    def _():
        pl.semaphore_signal(barrier, inc=1, device_id={"seq": me + 1}, device_id_type=MESH)

    pl.semaphore_wait(barrier, has_left.astype(jnp.int32) + has_right.astype(jnp.int32))

    def to_right(source, index):
        return pltpu.make_async_remote_copy(
            src_ref=source,
            dst_ref=shards.at[index],
            send_sem=right_sem.at[index],
            recv_sem=recv_sem.at[index],
            device_id={"seq": me + 1},
            device_id_type=MESH,
        )

    def to_left(source, index):
        return pltpu.make_async_remote_copy(
            src_ref=source,
            dst_ref=shards.at[index],
            send_sem=left_sem.at[index],
            recv_sem=recv_sem.at[index],
            device_id={"seq": me - 1},
            device_id_type=MESH,
        )

    @pl.when(has_right)
    def _():
        to_right(tok_ref, me).start()

    @pl.when(has_left)
    def _():
        to_left(tok_ref, me).start()

    shards[me] = tok_ref[...]
    lane = lax.broadcasted_iota(jnp.int32, (rows, pair), 1)
    first = lane < head_dim
    top[...] = jnp.full(top.shape, -jnp.inf, jnp.float32)
    total[...] = jnp.zeros(total.shape, jnp.float32)
    acc[...] = jnp.zeros(acc.shape, jnp.float32)
    load_in.wait()
    own = normalize(tok_ref[...].astype(jnp.float32), gain_ref[...]).astype(jnp.bfloat16)
    for p in range(pairs):
        part = jnp.dot(
            own, win[:, p * pair : (p + 1) * pair], preferred_element_type=jnp.float32
        ).astype(jnp.bfloat16)
        part = part * jnp.bfloat16(head_dim ** (-0.5))
        query2[p, 0:rows] = jnp.where(first, part, jnp.zeros_like(part))
        query2[p, rows : 2 * rows] = jnp.where(first, jnp.zeros_like(part), part)

    def absorb(index):
        normed = normalize(shards[index].astype(jnp.float32), gain_ref[...]).astype(jnp.bfloat16)
        block = min(256, width)
        for c in range(2 * width // block):
            kv[:, c * block : (c + 1) * block] = jnp.dot(
                normed,
                win[:, width + c * block : width + (c + 1) * block],
                preferred_element_type=jnp.float32,
            ).astype(jnp.bfloat16)
        for p in range(pairs):
            keys = kv[:, p * pair : (p + 1) * pair]
            values = kv[:, width + p * pair : width + (p + 1) * pair]
            scores = lax.dot_general(
                query2[p], keys, (((1,), (1,)), ((), ())), preferred_element_type=jnp.float32
            )
            old = top[p][:, 0:1]
            new = jnp.maximum(old, jnp.max(scores, -1, keepdims=True))
            scale = jnp.exp(old - new)
            weights = jnp.exp(scores - new)
            total[p] = jnp.broadcast_to(
                total[p][:, 0:1] * scale + jnp.sum(weights, -1, keepdims=True), total.shape[1:]
            )
            top[p] = jnp.broadcast_to(new, top.shape[1:])
            acc[p] = acc[p] * scale + jnp.dot(
                weights.astype(jnp.bfloat16), values, preferred_element_type=jnp.float32
            )

    def step(distance, carry):
        low, high = me - distance, me + distance

        @pl.when((distance > 0) & (low >= 0))
        def _():
            to_left(shards.at[low], low).wait_recv()

            @pl.when(has_right)
            def _():
                to_right(shards.at[low], low).start()

        @pl.when((distance > 0) & (high < ranks))
        def _():
            to_right(shards.at[high], high).wait_recv()

            @pl.when(has_left)
            def _():
                to_left(shards.at[high], high).start()

        def side(which, inner):
            index = jnp.where(which == 0, low, high)

            @pl.when((index >= 0) & (index < ranks) & ((distance > 0) | (which == 0)))
            def _():
                absorb(index)

            return inner

        lax.fori_loop(0, 2, side, 0)
        return carry

    lax.fori_loop(0, ranks, step, 0)
    for p in range(pairs):
        even = acc[p, 0:rows] / total[p, 0:rows]
        odd = acc[p, rows : 2 * rows] / total[p, rows : 2 * rows]
        context[:, p * pair : (p + 1) * pair] = jnp.where(first, even, odd).astype(jnp.bfloat16)
    load_out.wait()
    hidden = tok_ref[...].astype(jnp.float32) + jnp.dot(
        context[...], wout[...], preferred_element_type=jnp.float32
    )
    hidden_ref[...] = hidden
    normed2_ref[...] = normalize(hidden, gain2_ref[...]).astype(jnp.bfloat16)

    def drain(index, carry):
        @pl.when(has_right & (index <= me))
        def _():
            to_right(shards.at[index], index).wait_send()

        @pl.when(has_left & (index >= me))
        def _():
            to_left(shards.at[index], index).wait_send()

        return carry

    lax.fori_loop(0, ranks, drain, 0)


def attention(tokens, attn_in, attn_out, gain_attn, gain_expert):
    rows, width = tokens.shape
    ranks = lax.axis_size("seq")
    head_dim = width // HEADS
    pair = 2 * head_dim
    pairs = width // pair
    vmem = pl.BlockSpec(memory_space=pltpu.VMEM)
    hbm = pl.BlockSpec(memory_space=pl.ANY)
    return pl.pallas_call(
        functools.partial(attention_kernel, ranks, head_dim),
        out_shape=(
            jax.ShapeDtypeStruct((rows, width), jnp.float32),
            jax.ShapeDtypeStruct((rows, width), jnp.bfloat16),
        ),
        in_specs=[vmem, hbm, hbm, vmem, vmem],
        out_specs=(vmem, vmem),
        scratch_shapes=[
            pltpu.VMEM((ranks, rows, width), jnp.bfloat16),
            pltpu.VMEM(attn_in.shape, jnp.bfloat16),
            pltpu.VMEM(attn_out.shape, jnp.bfloat16),
            pltpu.VMEM((pairs, 2 * rows, pair), jnp.bfloat16),
            pltpu.VMEM((rows, 2 * width), jnp.bfloat16),
            pltpu.VMEM((pairs, 2 * rows, pair), jnp.float32),
            pltpu.VMEM((pairs, 2 * rows, pair), jnp.float32),
            pltpu.VMEM((pairs, 2 * rows, pair), jnp.float32),
            pltpu.VMEM((rows, width), jnp.bfloat16),
            pltpu.SemaphoreType.DMA((2,)),
            pltpu.SemaphoreType.DMA((ranks,)),
            pltpu.SemaphoreType.DMA((ranks,)),
            pltpu.SemaphoreType.DMA((ranks,)),
        ],
        compiler_params=pltpu.CompilerParams(
            collective_id=0, has_side_effects=True, vmem_limit_bytes=VMEM_LIMIT
        ),
    )(tokens, attn_in, attn_out, gain_attn[None, :], gain_expert[None, :])


def expert_kernel(
    sizes,
    rows_ref,
    w1_hbm,
    w2_hbm,
    back_ref,
    arrived,
    result,
    inner,
    w1,
    w2,
    w_sem,
    out_sem,
    in_sem,
    reply_sem,
    back_sem,
):
    secs, grps, ranks = sizes
    groups = secs * grps
    devices, most, width = rows_ref.shape
    hidden_units = w1.shape[1]
    sec, grp, me = lax.axis_index("sec"), lax.axis_index("grp"), lax.axis_index("seq")
    group = sec * grps + grp
    flat = group * ranks + me
    load1 = pltpu.make_async_copy(w1_hbm, w1, w_sem.at[0])
    load2 = pltpu.make_async_copy(w2_hbm, w2, w_sem.at[1])
    load1.start()
    load2.start()
    barrier = pltpu.get_barrier_semaphore()

    def place(other_group, other_rank):
        return (other_group // grps, other_group % grps, other_rank)

    def greet(offset, carry):
        other = (flat + offset) % devices
        pl.semaphore_signal(
            barrier, inc=1, device_id=place(other // ranks, other % ranks), device_id_type=MESH
        )
        return carry

    lax.fori_loop(1, devices, greet, 0)
    pl.semaphore_wait(barrier, devices - 1)

    def send(other_group, other_rank):
        return pltpu.make_async_remote_copy(
            src_ref=rows_ref.at[other_group * ranks + other_rank],
            dst_ref=arrived.at[me, group],
            send_sem=out_sem.at[other_rank, other_group],
            recv_sem=in_sem.at[me, group],
            device_id=place(other_group, other_rank),
            device_id_type=MESH,
        )

    def receive(other_group, other_rank):
        return pltpu.make_async_remote_copy(
            src_ref=rows_ref.at[flat],
            dst_ref=arrived.at[other_rank, other_group],
            send_sem=out_sem.at[other_rank, other_group],
            recv_sem=in_sem.at[other_rank, other_group],
            device_id=place(other_group, other_rank),
            device_id_type=MESH,
        )

    def reply(other_group, other_rank):
        return pltpu.make_async_remote_copy(
            src_ref=result.at[other_rank, other_group],
            dst_ref=back_ref.at[flat],
            send_sem=reply_sem.at[other_rank, other_group],
            recv_sem=back_sem.at[flat],
            device_id=place(other_group, other_rank),
            device_id_type=MESH,
        )

    def returned(other_group, other_rank):
        other = other_group * ranks + other_rank
        return pltpu.make_async_remote_copy(
            src_ref=result.at[other_rank, other_group],
            dst_ref=back_ref.at[other],
            send_sem=reply_sem.at[other_rank, other_group],
            recv_sem=back_sem.at[other],
            device_id=place(other_group, other_rank),
            device_id_type=MESH,
        )

    def over_groups(rank, act):
        def one(offset, carry):
            other_group = (group + offset) % groups

            @pl.when((offset > 0) | (rank != me))
            def _():
                act(other_group, rank)

            return carry

        lax.fori_loop(0, groups, one, 0)

    def by_distance(act):
        def one(step, carry):
            distance = (step + 1) // 2
            rank = jnp.where(step % 2 == 1, me - distance, me + distance)

            @pl.when((rank >= 0) & (rank < ranks))
            def _():
                act(rank)

            return carry

        lax.fori_loop(0, 2 * ranks - 1, one, 0)

    by_distance(lambda rank: over_groups(rank, lambda g, r: send(g, r).start()))
    arrived[me, group] = rows_ref[flat]
    load1.wait()
    load2.wait()
    block = 256 if hidden_units % 256 == 0 else hidden_units
    out_block = 256 if width % 256 == 0 else width

    def work(rank):
        over_groups(rank, lambda g, r: receive(g, r).wait_recv())
        rows = arrived[rank].reshape(groups * most, width)
        for c in range(0, hidden_units, block):
            inner[:, c : c + block] = jax.nn.relu(
                jnp.dot(rows, w1[:, c : c + block], preferred_element_type=jnp.float32)
            ).astype(jnp.bfloat16)
        for c in range(0, width, out_block):
            result[rank, :, :, c : c + out_block] = (
                jnp.dot(inner[...], w2[:, c : c + out_block], preferred_element_type=jnp.float32)
                .astype(jnp.bfloat16)
                .reshape(groups, most, out_block)
            )
        over_groups(rank, lambda g, r: reply(g, r).start())

    by_distance(work)
    back_ref[flat] = result[me, group]
    by_distance(lambda rank: over_groups(rank, lambda g, r: send(g, r).wait_send()))
    by_distance(lambda rank: over_groups(rank, lambda g, r: returned(g, r).wait_recv()))
    by_distance(lambda rank: over_groups(rank, lambda g, r: reply(g, r).wait_send()))


def run_experts(rows, w1, w2):
    devices, most, width = rows.shape
    sizes = tuple(lax.axis_size(name) for name in AXES)
    groups, ranks = sizes[0] * sizes[1], sizes[2]
    vmem = pl.BlockSpec(memory_space=pltpu.VMEM)
    hbm = pl.BlockSpec(memory_space=pl.ANY)
    return pl.pallas_call(
        functools.partial(expert_kernel, sizes),
        out_shape=jax.ShapeDtypeStruct(rows.shape, jnp.bfloat16),
        in_specs=[vmem, hbm, hbm],
        out_specs=vmem,
        scratch_shapes=[
            pltpu.VMEM((ranks, groups, most, width), jnp.bfloat16),
            pltpu.VMEM((ranks, groups, most, width), jnp.bfloat16),
            pltpu.VMEM((groups * most, w1.shape[1]), jnp.bfloat16),
            pltpu.VMEM(w1.shape, jnp.bfloat16),
            pltpu.VMEM(w2.shape, jnp.bfloat16),
            pltpu.SemaphoreType.DMA((2,)),
            pltpu.SemaphoreType.DMA((ranks, groups)),
            pltpu.SemaphoreType.DMA((ranks, groups)),
            pltpu.SemaphoreType.DMA((ranks, groups)),
            pltpu.SemaphoreType.DMA((devices,)),
        ],
        compiler_params=pltpu.CompilerParams(
            collective_id=1, has_side_effects=True, vmem_limit_bytes=VMEM_LIMIT
        ),
    )(rows, w1, w2)


def body(
    tokens, expert_ids, attn_in, attn_out, gain_attn, gain_expert, router, expert_in, expert_out
):
    tok_rows, model_width = tokens.shape
    hidden, normed2 = attention(tokens, attn_in, attn_out, gain_attn, gain_expert)
    experts = lax.axis_size(AXES) * expert_in.shape[0]
    most_rows = max(2, 2 * tok_rows // experts)
    picked = expert_ids[:, 0]
    one_hot = (picked[:, None] == jnp.arange(experts, dtype=jnp.int32)[None, :]).astype(jnp.int32)
    earlier = jnp.sum((jnp.cumsum(one_hot, 0) - one_hot) * one_hot, 1)
    dest_slot = picked * most_rows + earlier
    route = (
        dest_slot[:, None] == jnp.arange(experts * most_rows, dtype=jnp.int32)[None, :]
    ).astype(jnp.bfloat16)
    outgoing = jnp.einsum("ts,td->sd", route, normed2, preferred_element_type=jnp.float32).astype(
        jnp.bfloat16
    )
    logits = jnp.dot(normed2, router, preferred_element_type=jnp.float32)
    gate_value = jax.nn.sigmoid(jnp.sum(logits * one_hot.astype(jnp.float32), 1))
    send_rows = outgoing.reshape(experts, most_rows, model_width)
    back_rows = run_experts(send_rows, expert_in[0], expert_out[0])
    returned = back_rows.reshape(experts * most_rows, model_width)
    combined = jnp.dot(route, returned, preferred_element_type=jnp.float32)
    return (hidden + gate_value[:, None] * combined).astype(jnp.bfloat16)


def solution(mesh):
    return jax.shard_map(
        body,
        mesh=mesh,
        in_specs=(P(AXES, None), P(AXES, None), P(), P(), P(), P(), P(), P(AXES, None, None), P(AXES, None, None)),
        out_specs=P(AXES, None),
        check_vma=False,
    )
```

```python
import functools

import jax
import jax.numpy as jnp
from jax import lax
from jax.experimental import pallas as pl
from jax.experimental.pallas import tpu as pltpu
from jax.sharding import PartitionSpec as P

HEADS = 16
AXES = ("sec", "grp", "seq")
MESH = pl.DeviceIdType.MESH
VMEM_LIMIT = 60 * 1024 * 1024


def normalize(values, gain):
    return values * lax.rsqrt(jnp.mean(values * values, -1, keepdims=True) + 1e-06) * gain


def layer_kernel(
    sizes,
    head_dim,
    tok_ref,
    ids_ref,
    ids_row_ref,
    win_hbm,
    wout_hbm,
    gain_ref,
    gain2_ref,
    router_ref,
    w1_hbm,
    w2_hbm,
    out_ref,
    shards,
    win,
    wout,
    query2,
    kv,
    acc,
    top,
    total,
    context,
    rows_buf,
    arrived,
    result,
    back,
    inner,
    w1,
    w2,
    hidden_buf,
    normed2_buf,
    combined,
    w_sem,
    right_sem,
    left_sem,
    recv_sem,
    out_sem,
    in_sem,
    reply_sem,
    back_sem,
):
    secs, grps, ranks = sizes
    groups = secs * grps
    devices = groups * ranks
    most = rows_buf.shape[2]
    rows, width = tok_ref.shape
    pair = 2 * head_dim
    pairs = width // pair
    me = lax.axis_index("seq")
    load_in = pltpu.make_async_copy(win_hbm, win, w_sem.at[0])
    load_out = pltpu.make_async_copy(wout_hbm, wout, w_sem.at[1])
    load_in.start()
    load_out.start()
    load1 = pltpu.make_async_copy(w1_hbm, w1, w_sem.at[2])
    load2 = pltpu.make_async_copy(w2_hbm, w2, w_sem.at[3])
    load1.start()
    load2.start()
    sec, grp = lax.axis_index("sec"), lax.axis_index("grp")
    group = sec * grps + grp
    flat = group * ranks + me
    has_left, has_right = me > 0, me < ranks - 1
    barrier = pltpu.get_barrier_semaphore()

    def place(other_group, other_rank):
        return (other_group // grps, other_group % grps, other_rank)

    def greet(offset, carry):
        other = (flat + offset) % devices
        pl.semaphore_signal(
            barrier, inc=1, device_id=place(other // ranks, other % ranks), device_id_type=MESH
        )
        return carry

    lax.fori_loop(1, devices, greet, 0)
    pl.semaphore_wait(barrier, devices - 1)

    def to_right(source, index):
        return pltpu.make_async_remote_copy(
            src_ref=source,
            dst_ref=shards.at[index],
            send_sem=right_sem.at[index],
            recv_sem=recv_sem.at[index],
            device_id={"seq": me + 1},
            device_id_type=MESH,
        )

    def to_left(source, index):
        return pltpu.make_async_remote_copy(
            src_ref=source,
            dst_ref=shards.at[index],
            send_sem=left_sem.at[index],
            recv_sem=recv_sem.at[index],
            device_id={"seq": me - 1},
            device_id_type=MESH,
        )

    @pl.when(has_right)
    def _():
        to_right(tok_ref, me).start()

    @pl.when(has_left)
    def _():
        to_left(tok_ref, me).start()

    shards[me] = tok_ref[...]
    experts = devices
    ids = ids_ref[...].astype(jnp.float32)
    ids_row = ids_row_ref[...].astype(jnp.float32)
    chosen = (
        lax.broadcasted_iota(jnp.int32, (rows, experts), 1).astype(jnp.float32) == ids
    ).astype(jnp.float32)
    chosen_row = (
        lax.broadcasted_iota(jnp.int32, (experts, rows), 0).astype(jnp.float32) == ids_row
    ).astype(jnp.float32)
    down = lax.broadcasted_iota(jnp.int32, (rows, rows), 0)
    across = lax.broadcasted_iota(jnp.int32, (rows, rows), 1)
    below = (across < down).astype(jnp.float32).astype(jnp.bfloat16)
    above = (down < across).astype(jnp.float32).astype(jnp.bfloat16)
    earlier = jnp.dot(below, chosen.astype(jnp.bfloat16), preferred_element_type=jnp.float32)
    slot_column = ids * most + jnp.sum(earlier * chosen, 1, keepdims=True)
    earlier_row = jnp.dot(chosen_row.astype(jnp.bfloat16), above, preferred_element_type=jnp.float32)
    slot_row = ids_row * most + jnp.sum(earlier_row * chosen_row, 0, keepdims=True)
    lane = lax.broadcasted_iota(jnp.int32, (rows, pair), 1)
    first = lane < head_dim
    top[...] = jnp.full(top.shape, -jnp.inf, jnp.float32)
    total[...] = jnp.zeros(total.shape, jnp.float32)
    acc[...] = jnp.zeros(acc.shape, jnp.float32)
    load_in.wait()
    own = normalize(tok_ref[...].astype(jnp.float32), gain_ref[...]).astype(jnp.bfloat16)
    for p in range(pairs):
        part = jnp.dot(
            own, win[:, p * pair : (p + 1) * pair], preferred_element_type=jnp.float32
        ).astype(jnp.bfloat16)
        part = part * jnp.bfloat16(head_dim ** (-0.5))
        query2[p, 0:rows] = jnp.where(first, part, jnp.zeros_like(part))
        query2[p, rows : 2 * rows] = jnp.where(first, jnp.zeros_like(part), part)

    def absorb(index):
        normed = normalize(shards[index].astype(jnp.float32), gain_ref[...]).astype(jnp.bfloat16)
        block = min(256, width)
        for c in range(2 * width // block):
            kv[:, c * block : (c + 1) * block] = jnp.dot(
                normed,
                win[:, width + c * block : width + (c + 1) * block],
                preferred_element_type=jnp.float32,
            ).astype(jnp.bfloat16)
        for p in range(pairs):
            keys = kv[:, p * pair : (p + 1) * pair]
            values = kv[:, width + p * pair : width + (p + 1) * pair]
            scores = lax.dot_general(
                query2[p], keys, (((1,), (1,)), ((), ())), preferred_element_type=jnp.float32
            )
            old = top[p][:, 0:1]
            new = jnp.maximum(old, jnp.max(scores, -1, keepdims=True))
            scale = jnp.exp(old - new)
            weights = jnp.exp(scores - new)
            total[p] = jnp.broadcast_to(
                total[p][:, 0:1] * scale + jnp.sum(weights, -1, keepdims=True), total.shape[1:]
            )
            top[p] = jnp.broadcast_to(new, top.shape[1:])
            acc[p] = acc[p] * scale + jnp.dot(
                weights.astype(jnp.bfloat16), values, preferred_element_type=jnp.float32
            )

    def step(distance, carry):
        low, high = me - distance, me + distance

        @pl.when((distance > 0) & (low >= 0))
        def _():
            to_left(shards.at[low], low).wait_recv()

            @pl.when(has_right)
            def _():
                to_right(shards.at[low], low).start()

        @pl.when((distance > 0) & (high < ranks))
        def _():
            to_right(shards.at[high], high).wait_recv()

            @pl.when(has_left)
            def _():
                to_left(shards.at[high], high).start()

        def side(which, inner):
            index = jnp.where(which == 0, low, high)

            @pl.when((index >= 0) & (index < ranks) & ((distance > 0) | (which == 0)))
            def _():
                absorb(index)

            return inner

        lax.fori_loop(0, 2, side, 0)
        return carry

    lax.fori_loop(0, ranks, step, 0)
    for p in range(pairs):
        even = acc[p, 0:rows] / total[p, 0:rows]
        odd = acc[p, rows : 2 * rows] / total[p, rows : 2 * rows]
        context[:, p * pair : (p + 1) * pair] = jnp.where(first, even, odd).astype(jnp.bfloat16)
    load_out.wait()
    hidden = tok_ref[...].astype(jnp.float32) + jnp.dot(
        context[...], wout[...], preferred_element_type=jnp.float32
    )
    hidden_buf[...] = hidden
    normed2_buf[...] = normalize(hidden, gain2_ref[...]).astype(jnp.bfloat16)

    def send(other_group, other_rank):
        return pltpu.make_async_remote_copy(
            src_ref=rows_buf.at[other_rank, other_group],
            dst_ref=arrived.at[me, group],
            send_sem=out_sem.at[other_rank, other_group],
            recv_sem=in_sem.at[me, group],
            device_id=place(other_group, other_rank),
            device_id_type=MESH,
        )

    def receive(other_group, other_rank):
        return pltpu.make_async_remote_copy(
            src_ref=rows_buf.at[me, group],
            dst_ref=arrived.at[other_rank, other_group],
            send_sem=out_sem.at[other_rank, other_group],
            recv_sem=in_sem.at[other_rank, other_group],
            device_id=place(other_group, other_rank),
            device_id_type=MESH,
        )

    def reply(other_group, other_rank):
        return pltpu.make_async_remote_copy(
            src_ref=result.at[other_rank, other_group],
            dst_ref=back.at[me, group],
            send_sem=reply_sem.at[other_rank, other_group],
            recv_sem=back_sem.at[me, group],
            device_id=place(other_group, other_rank),
            device_id_type=MESH,
        )

    def returned(other_group, other_rank):
        return pltpu.make_async_remote_copy(
            src_ref=result.at[other_rank, other_group],
            dst_ref=back.at[other_rank, other_group],
            send_sem=reply_sem.at[other_rank, other_group],
            recv_sem=back_sem.at[other_rank, other_group],
            device_id=place(other_group, other_rank),
            device_id_type=MESH,
        )

    def over_groups(rank, act):
        def one(offset, carry):
            other_group = (group + offset) % groups

            @pl.when((offset > 0) | (rank != me))
            def _():
                act(other_group, rank)

            return carry

        lax.fori_loop(0, groups, one, 0)

    def farthest_first(act):
        def one(step, carry):
            place_in_line = 2 * ranks - 2 - step
            distance = (place_in_line + 1) // 2
            rank = jnp.where(place_in_line % 2 == 1, me - distance, me + distance)

            @pl.when((rank >= 0) & (rank < ranks))
            def _():
                act(rank)

            return carry

        lax.fori_loop(0, 2 * ranks - 1, one, 0)

    def middle_first(act):
        def one(step, carry):
            distance = step // 2
            low = (ranks - 1) // 2
            near = jnp.where(step % 2 == 0, low - distance, low + 1 + distance)
            rank = jnp.where(2 * me >= ranks, ranks - 1 - near, near)

            @pl.when((rank >= 0) & (rank < ranks))
            def _():
                act(rank)

            return carry

        lax.fori_loop(0, ranks + 1, one, 0)

    slots = groups * most

    def label(rank, shape, dim):
        column = lax.broadcasted_iota(jnp.int32, shape, dim).astype(jnp.float32)
        block = jnp.floor((column + 0.5) * (1.0 / most))
        return (block * ranks + rank.astype(jnp.float32)) * most + (column - block * most)

    def scatter(rank):
        pick = (label(rank, (slots, rows), 0) == slot_row).astype(jnp.float32).astype(jnp.bfloat16)
        rows_buf[rank] = (
            jnp.dot(pick, normed2_buf[...], preferred_element_type=jnp.float32)
            .astype(jnp.bfloat16)
            .reshape(groups, most, width)
        )
        over_groups(rank, lambda g, r: send(g, r).start())

    farthest_first(scatter)
    arrived[me, group] = rows_buf[me, group]
    logits = jnp.dot(normed2_buf[...], router_ref[...], preferred_element_type=jnp.float32)
    gate = jax.nn.sigmoid(jnp.sum(logits * chosen, 1, keepdims=True))
    load1.wait()
    load2.wait()
    hidden_units = w1.shape[1]
    block = 256 if hidden_units % 256 == 0 else hidden_units
    out_block = 256 if width % 256 == 0 else width

    def work(rank):
        over_groups(rank, lambda g, r: receive(g, r).wait_recv())
        batch = arrived[rank].reshape(slots, width)
        for c in range(0, hidden_units, block):
            inner[:, c : c + block] = jax.nn.relu(
                jnp.dot(batch, w1[:, c : c + block], preferred_element_type=jnp.float32)
            ).astype(jnp.bfloat16)
        for c in range(0, width, out_block):
            result[rank, :, :, c : c + out_block] = (
                jnp.dot(inner[...], w2[:, c : c + out_block], preferred_element_type=jnp.float32)
                .astype(jnp.bfloat16)
                .reshape(groups, most, out_block)
            )
        over_groups(rank, lambda g, r: reply(g, r).start())

    middle_first(work)
    back[me, group] = result[me, group]
    combined[...] = jnp.zeros(combined.shape, jnp.float32)

    def gather(rank):
        over_groups(rank, lambda g, r: returned(g, r).wait_recv())
        pick = (label(rank, (rows, slots), 1) == slot_column).astype(jnp.float32).astype(jnp.bfloat16)
        combined[...] += jnp.dot(
            pick, back[rank].reshape(slots, width), preferred_element_type=jnp.float32
        )

    middle_first(gather)
    out_ref[...] = (hidden_buf[...] + gate * combined[...]).astype(jnp.bfloat16)
    farthest_first(lambda rank: over_groups(rank, lambda g, r: send(g, r).wait_send()))
    farthest_first(lambda rank: over_groups(rank, lambda g, r: reply(g, r).wait_send()))

    def drain(index, carry):
        @pl.when(has_right & (index <= me))
        def _():
            to_right(shards.at[index], index).wait_send()

        @pl.when(has_left & (index >= me))
        def _():
            to_left(shards.at[index], index).wait_send()

        return carry

    lax.fori_loop(0, ranks, drain, 0)


def layer(tokens, expert_ids, attn_in, attn_out, gain_attn, gain_expert, router, w1, w2):
    rows, width = tokens.shape
    sizes = tuple(lax.axis_size(name) for name in AXES)
    groups, ranks = sizes[0] * sizes[1], sizes[2]
    devices = groups * ranks
    most = max(2, 2 * rows // devices)
    head_dim = width // HEADS
    pair = 2 * head_dim
    pairs = width // pair
    vmem = pl.BlockSpec(memory_space=pltpu.VMEM)
    hbm = pl.BlockSpec(memory_space=pl.ANY)
    blocks = pltpu.VMEM((ranks, groups, most, width), jnp.bfloat16)
    per_device = pltpu.SemaphoreType.DMA((ranks, groups))
    return pl.pallas_call(
        functools.partial(layer_kernel, sizes, head_dim),
        out_shape=jax.ShapeDtypeStruct((rows, width), jnp.bfloat16),
        in_specs=[vmem, vmem, vmem, hbm, hbm, vmem, vmem, vmem, hbm, hbm],
        out_specs=vmem,
        scratch_shapes=[
            pltpu.VMEM((ranks, rows, width), jnp.bfloat16),
            pltpu.VMEM(attn_in.shape, jnp.bfloat16),
            pltpu.VMEM(attn_out.shape, jnp.bfloat16),
            pltpu.VMEM((pairs, 2 * rows, pair), jnp.bfloat16),
            pltpu.VMEM((rows, 2 * width), jnp.bfloat16),
            pltpu.VMEM((pairs, 2 * rows, pair), jnp.float32),
            pltpu.VMEM((pairs, 2 * rows, pair), jnp.float32),
            pltpu.VMEM((pairs, 2 * rows, pair), jnp.float32),
            pltpu.VMEM((rows, width), jnp.bfloat16),
            blocks,
            blocks,
            blocks,
            blocks,
            pltpu.VMEM((groups * most, w1.shape[1]), jnp.bfloat16),
            pltpu.VMEM(w1.shape, jnp.bfloat16),
            pltpu.VMEM(w2.shape, jnp.bfloat16),
            pltpu.VMEM((rows, width), jnp.float32),
            pltpu.VMEM((rows, width), jnp.bfloat16),
            pltpu.VMEM((rows, width), jnp.float32),
            pltpu.SemaphoreType.DMA((4,)),
            pltpu.SemaphoreType.DMA((ranks,)),
            pltpu.SemaphoreType.DMA((ranks,)),
            pltpu.SemaphoreType.DMA((ranks,)),
            per_device,
            per_device,
            per_device,
            per_device,
        ],
        compiler_params=pltpu.CompilerParams(
            collective_id=0, has_side_effects=True, vmem_limit_bytes=VMEM_LIMIT
        ),
    )(
        tokens,
        expert_ids,
        expert_ids.reshape(1, rows),
        attn_in,
        attn_out,
        gain_attn[None, :],
        gain_expert[None, :],
        router,
        w1,
        w2,
    )


def body(
    tokens, expert_ids, attn_in, attn_out, gain_attn, gain_expert, router, expert_in, expert_out
):
    return layer(
        tokens,
        expert_ids,
        attn_in,
        attn_out,
        gain_attn,
        gain_expert,
        router,
        expert_in[0],
        expert_out[0],
    )


def solution(mesh):
    return jax.shard_map(
        body,
        mesh=mesh,
        in_specs=(P(AXES, None), P(AXES, None), P(), P(), P(), P(), P(), P(AXES, None, None), P(AXES, None, None)),
        out_specs=P(AXES, None),
        check_vma=False,
    )
```

```python
import functools

import jax
import jax.numpy as jnp
from jax import lax
from jax.experimental import pallas as pl
from jax.experimental.pallas import tpu as pltpu
from jax.sharding import PartitionSpec as P

HEADS = 16
AXES = ("sec", "grp", "seq")
MESH = pl.DeviceIdType.MESH
VMEM_LIMIT = 60 * 1024 * 1024


def normalize(values, gain):
    return values * lax.rsqrt(jnp.mean(values * values, -1, keepdims=True) + 1e-06) * gain


def layer_kernel(
    sizes,
    head_dim,
    tok_ref,
    ids_row_ref,
    win_hbm,
    wout_hbm,
    gain_ref,
    gain2_ref,
    router_ref,
    w1_hbm,
    w2_hbm,
    out_ref,
    shards,
    win,
    wout,
    query2,
    kv,
    acc,
    top,
    total,
    context,
    rows_buf,
    arrived,
    result,
    back,
    inner,
    w1,
    w2,
    hidden_buf,
    normed2_buf,
    combined,
    w_sem,
    right_sem,
    left_sem,
    recv_sem,
    out_sem,
    in_sem,
    reply_sem,
    back_sem,
):
    secs, grps, ranks = sizes
    groups = secs * grps
    devices = groups * ranks
    most = rows_buf.shape[2]
    rows, width = tok_ref.shape
    pair = 2 * head_dim
    pairs = width // pair
    me = lax.axis_index("seq")
    load_in = pltpu.make_async_copy(win_hbm, win, w_sem.at[0])
    load_out = pltpu.make_async_copy(wout_hbm, wout, w_sem.at[1])
    load_in.start()
    load_out.start()
    load1 = pltpu.make_async_copy(w1_hbm, w1, w_sem.at[2])
    load2 = pltpu.make_async_copy(w2_hbm, w2, w_sem.at[3])
    load1.start()
    load2.start()
    sec, grp = lax.axis_index("sec"), lax.axis_index("grp")
    group = sec * grps + grp
    flat = group * ranks + me
    has_left, has_right = me > 0, me < ranks - 1
    barrier = pltpu.get_barrier_semaphore()

    def place(other_group, other_rank):
        return (other_group // grps, other_group % grps, other_rank)

    def greet(offset, carry):
        other = (flat + offset) % devices
        pl.semaphore_signal(
            barrier, inc=1, device_id=place(other // ranks, other % ranks), device_id_type=MESH
        )
        return carry

    lax.fori_loop(1, devices, greet, 0)
    pl.semaphore_wait(barrier, devices - 1)

    def to_right(source, index):
        return pltpu.make_async_remote_copy(
            src_ref=source,
            dst_ref=shards.at[index],
            send_sem=right_sem.at[index],
            recv_sem=recv_sem.at[index],
            device_id={"seq": me + 1},
            device_id_type=MESH,
        )

    def to_left(source, index):
        return pltpu.make_async_remote_copy(
            src_ref=source,
            dst_ref=shards.at[index],
            send_sem=left_sem.at[index],
            recv_sem=recv_sem.at[index],
            device_id={"seq": me - 1},
            device_id_type=MESH,
        )

    @pl.when(has_right)
    def _():
        to_right(tok_ref, me).start()

    @pl.when(has_left)
    def _():
        to_left(tok_ref, me).start()

    shards[me] = tok_ref[...]
    experts = devices
    ids_row = ids_row_ref[...].astype(jnp.float32)
    chosen_row = (
        lax.broadcasted_iota(jnp.int32, (experts, rows), 0).astype(jnp.float32) == ids_row
    ).astype(jnp.float32)
    down = lax.broadcasted_iota(jnp.int32, (rows, rows), 0)
    across = lax.broadcasted_iota(jnp.int32, (rows, rows), 1)
    ids = jnp.sum(jnp.where(down == across, ids_row, 0.0), 1, keepdims=True)
    chosen = (
        lax.broadcasted_iota(jnp.int32, (rows, experts), 1).astype(jnp.float32) == ids
    ).astype(jnp.float32)
    below = (across < down).astype(jnp.float32).astype(jnp.bfloat16)
    above = (down < across).astype(jnp.float32).astype(jnp.bfloat16)
    earlier = jnp.dot(below, chosen.astype(jnp.bfloat16), preferred_element_type=jnp.float32)
    slot_column = ids * most + jnp.sum(earlier * chosen, 1, keepdims=True)
    earlier_row = jnp.dot(chosen_row.astype(jnp.bfloat16), above, preferred_element_type=jnp.float32)
    slot_row = ids_row * most + jnp.sum(earlier_row * chosen_row, 0, keepdims=True)
    lane = lax.broadcasted_iota(jnp.int32, (rows, pair), 1)
    first = lane < head_dim
    top[...] = jnp.full(top.shape, -jnp.inf, jnp.float32)
    total[...] = jnp.zeros(total.shape, jnp.float32)
    acc[...] = jnp.zeros(acc.shape, jnp.float32)
    load_in.wait()
    own = normalize(tok_ref[...].astype(jnp.float32), gain_ref[...]).astype(jnp.bfloat16)
    for p in range(pairs):
        part = jnp.dot(
            own, win[:, p * pair : (p + 1) * pair], preferred_element_type=jnp.float32
        ).astype(jnp.bfloat16)
        part = part * jnp.bfloat16(head_dim ** (-0.5))
        query2[p, 0:rows] = jnp.where(first, part, jnp.zeros_like(part))
        query2[p, rows : 2 * rows] = jnp.where(first, jnp.zeros_like(part), part)

    def absorb(index):
        normed = normalize(shards[index].astype(jnp.float32), gain_ref[...]).astype(jnp.bfloat16)
        block = min(256, width)
        ones = jnp.ones((rows, pair), jnp.bfloat16)
        for c in range(2 * width // block):
            kv[:, c * block : (c + 1) * block] = jnp.dot(
                normed,
                win[:, width + c * block : width + (c + 1) * block],
                preferred_element_type=jnp.float32,
            ).astype(jnp.bfloat16)
        for p in range(pairs):
            keys = kv[:, p * pair : (p + 1) * pair]
            values = kv[:, width + p * pair : width + (p + 1) * pair]
            scores = lax.dot_general(
                query2[p], keys, (((1,), (1,)), ((), ())), preferred_element_type=jnp.float32
            )
            old = top[p]
            new = jnp.maximum(old, jnp.max(scores, -1, keepdims=True))
            scale = jnp.exp(old - new)
            spread = jnp.concatenate([new] * (rows // pair), 1) if rows % pair == 0 else new[:, 0:1]
            weights = jnp.exp(scores - spread).astype(jnp.bfloat16)
            update = jnp.dot(
                weights,
                jnp.concatenate([values, ones], 1),
                preferred_element_type=jnp.float32,
            )
            top[p] = new
            acc[p] = acc[p] * scale + update[:, 0:pair]
            total[p] = total[p] * scale + update[:, pair : 2 * pair]

    def step(distance, carry):
        low, high = me - distance, me + distance

        @pl.when((distance > 0) & (low >= 0))
        def _():
            to_left(shards.at[low], low).wait_recv()

            @pl.when(has_right)
            def _():
                to_right(shards.at[low], low).start()

        @pl.when((distance > 0) & (high < ranks))
        def _():
            to_right(shards.at[high], high).wait_recv()

            @pl.when(has_left)
            def _():
                to_left(shards.at[high], high).start()

        def side(which, inner):
            index = jnp.where(which == 0, low, high)

            @pl.when((index >= 0) & (index < ranks) & ((distance > 0) | (which == 0)))
            def _():
                absorb(index)

            return inner

        lax.fori_loop(0, 2, side, 0)
        return carry

    lax.fori_loop(0, ranks, step, 0)
    for p in range(pairs):
        even = acc[p, 0:rows] / total[p, 0:rows]
        odd = acc[p, rows : 2 * rows] / total[p, rows : 2 * rows]
        context[:, p * pair : (p + 1) * pair] = jnp.where(first, even, odd).astype(jnp.bfloat16)
    load_out.wait()
    hidden = tok_ref[...].astype(jnp.float32) + jnp.dot(
        context[...], wout[...], preferred_element_type=jnp.float32
    )
    hidden_buf[...] = hidden
    normed2_buf[...] = normalize(hidden, gain2_ref[...]).astype(jnp.bfloat16)

    def send(other_group, other_rank):
        return pltpu.make_async_remote_copy(
            src_ref=rows_buf.at[other_rank, other_group],
            dst_ref=arrived.at[me, group],
            send_sem=out_sem.at[other_rank, other_group],
            recv_sem=in_sem.at[me, group],
            device_id=place(other_group, other_rank),
            device_id_type=MESH,
        )

    def receive(other_group, other_rank):
        return pltpu.make_async_remote_copy(
            src_ref=rows_buf.at[me, group],
            dst_ref=arrived.at[other_rank, other_group],
            send_sem=out_sem.at[other_rank, other_group],
            recv_sem=in_sem.at[other_rank, other_group],
            device_id=place(other_group, other_rank),
            device_id_type=MESH,
        )

    def reply(other_group, other_rank):
        return pltpu.make_async_remote_copy(
            src_ref=result.at[other_rank, other_group],
            dst_ref=back.at[me, group],
            send_sem=reply_sem.at[other_rank, other_group],
            recv_sem=back_sem.at[me, group],
            device_id=place(other_group, other_rank),
            device_id_type=MESH,
        )

    def returned(other_group, other_rank):
        return pltpu.make_async_remote_copy(
            src_ref=result.at[other_rank, other_group],
            dst_ref=back.at[other_rank, other_group],
            send_sem=reply_sem.at[other_rank, other_group],
            recv_sem=back_sem.at[other_rank, other_group],
            device_id=place(other_group, other_rank),
            device_id_type=MESH,
        )

    def over_groups(rank, act):
        def one(offset, carry):
            other_group = (group + offset) % groups

            @pl.when((offset > 0) | (rank != me))
            def _():
                act(other_group, rank)

            return carry

        lax.fori_loop(0, groups, one, 0)

    def across_first(act):
        def one(step, carry):
            half = ranks // 2
            far = jnp.where(step < ranks - half, half + step, ranks - 1 - step)
            act(jnp.where(2 * me >= ranks, ranks - 1 - far, far))
            return carry

        lax.fori_loop(0, ranks, one, 0)

    def middle_first(act):
        def one(step, carry):
            distance = step // 2
            low = (ranks - 1) // 2
            near = jnp.where(step % 2 == 0, low - distance, low + 1 + distance)
            rank = jnp.where(2 * me >= ranks, ranks - 1 - near, near)

            @pl.when((rank >= 0) & (rank < ranks))
            def _():
                act(rank)

            return carry

        lax.fori_loop(0, ranks + 1, one, 0)

    slots = groups * most

    def label(rank, shape, dim):
        column = lax.broadcasted_iota(jnp.int32, shape, dim).astype(jnp.float32)
        block = jnp.floor((column + 0.5) * (1.0 / most))
        return (block * ranks + rank.astype(jnp.float32)) * most + (column - block * most)

    def scatter(rank):
        pick = (label(rank, (slots, rows), 0) == slot_row).astype(jnp.float32).astype(jnp.bfloat16)
        rows_buf[rank] = (
            jnp.dot(pick, normed2_buf[...], preferred_element_type=jnp.float32)
            .astype(jnp.bfloat16)
            .reshape(groups, most, width)
        )
        over_groups(rank, lambda g, r: send(g, r).start())

    across_first(scatter)
    arrived[me, group] = rows_buf[me, group]
    logits = lax.dot_general(
        normed2_buf[...],
        router_ref[...],
        (((1,), (1,)), ((), ())),
        preferred_element_type=jnp.float32,
    )
    gate = jax.nn.sigmoid(jnp.sum(logits * chosen, 1, keepdims=True))
    load1.wait()
    load2.wait()
    hidden_units = w1.shape[1]
    block = 256 if hidden_units % 256 == 0 else hidden_units
    out_block = 256 if width % 256 == 0 else width

    def work(rank):
        over_groups(rank, lambda g, r: receive(g, r).wait_recv())
        batch = arrived[rank].reshape(slots, width)
        for c in range(0, hidden_units, block):
            inner[:, c : c + block] = jax.nn.relu(
                jnp.dot(batch, w1[:, c : c + block], preferred_element_type=jnp.float32)
            ).astype(jnp.bfloat16)
        for c in range(0, width, out_block):
            result[rank, :, :, c : c + out_block] = (
                jnp.dot(inner[...], w2[:, c : c + out_block], preferred_element_type=jnp.float32)
                .astype(jnp.bfloat16)
                .reshape(groups, most, out_block)
            )
        over_groups(rank, lambda g, r: reply(g, r).start())

    middle_first(work)
    back[me, group] = result[me, group]
    combined[...] = jnp.zeros(combined.shape, jnp.float32)

    def gather(rank):
        over_groups(rank, lambda g, r: returned(g, r).wait_recv())
        pick = (label(rank, (rows, slots), 1) == slot_column).astype(jnp.float32).astype(jnp.bfloat16)
        combined[...] += jnp.dot(
            pick, back[rank].reshape(slots, width), preferred_element_type=jnp.float32
        )

    middle_first(gather)
    out_ref[...] = (hidden_buf[...] + gate * combined[...]).astype(jnp.bfloat16)
    across_first(lambda rank: over_groups(rank, lambda g, r: send(g, r).wait_send()))
    across_first(lambda rank: over_groups(rank, lambda g, r: reply(g, r).wait_send()))

    def drain(index, carry):
        @pl.when(has_right & (index <= me))
        def _():
            to_right(shards.at[index], index).wait_send()

        @pl.when(has_left & (index >= me))
        def _():
            to_left(shards.at[index], index).wait_send()

        return carry

    lax.fori_loop(0, ranks, drain, 0)


def layer(tokens, expert_ids, attn_in, attn_out, gain_attn, gain_expert, router, w1, w2):
    rows, width = tokens.shape
    sizes = tuple(lax.axis_size(name) for name in AXES)
    groups, ranks = sizes[0] * sizes[1], sizes[2]
    devices = groups * ranks
    most = max(2, 2 * rows // devices)
    head_dim = width // HEADS
    pair = 2 * head_dim
    pairs = width // pair
    vmem = pl.BlockSpec(memory_space=pltpu.VMEM)
    hbm = pl.BlockSpec(memory_space=pl.ANY)
    blocks = pltpu.VMEM((ranks, groups, most, width), jnp.bfloat16)
    per_device = pltpu.SemaphoreType.DMA((ranks, groups))
    return pl.pallas_call(
        functools.partial(layer_kernel, sizes, head_dim),
        out_shape=jax.ShapeDtypeStruct((rows, width), jnp.bfloat16),
        in_specs=[vmem, vmem, hbm, hbm, vmem, vmem, vmem, hbm, hbm],
        out_specs=vmem,
        scratch_shapes=[
            pltpu.VMEM((ranks, rows, width), jnp.bfloat16),
            pltpu.VMEM(attn_in.shape, jnp.bfloat16),
            pltpu.VMEM(attn_out.shape, jnp.bfloat16),
            pltpu.VMEM((pairs, 2 * rows, pair), jnp.bfloat16),
            pltpu.VMEM((rows, 2 * width), jnp.bfloat16),
            pltpu.VMEM((pairs, 2 * rows, pair), jnp.float32),
            pltpu.VMEM((pairs, 2 * rows, pair), jnp.float32),
            pltpu.VMEM((pairs, 2 * rows, pair), jnp.float32),
            pltpu.VMEM((rows, width), jnp.bfloat16),
            blocks,
            blocks,
            blocks,
            blocks,
            pltpu.VMEM((groups * most, w1.shape[1]), jnp.bfloat16),
            pltpu.VMEM(w1.shape, jnp.bfloat16),
            pltpu.VMEM(w2.shape, jnp.bfloat16),
            pltpu.VMEM((rows, width), jnp.float32),
            pltpu.VMEM((rows, width), jnp.bfloat16),
            pltpu.VMEM((rows, width), jnp.float32),
            pltpu.SemaphoreType.DMA((4,)),
            pltpu.SemaphoreType.DMA((ranks,)),
            pltpu.SemaphoreType.DMA((ranks,)),
            pltpu.SemaphoreType.DMA((ranks,)),
            per_device,
            per_device,
            per_device,
            per_device,
        ],
        compiler_params=pltpu.CompilerParams(
            collective_id=0, has_side_effects=True, vmem_limit_bytes=VMEM_LIMIT
        ),
    )(
        tokens,
        expert_ids.reshape(1, rows),
        attn_in,
        attn_out,
        gain_attn[None, :],
        gain_expert[None, :],
        router.T,
        w1,
        w2,
    )


def body(
    tokens, expert_ids, attn_in, attn_out, gain_attn, gain_expert, router, expert_in, expert_out
):
    return layer(
        tokens,
        expert_ids,
        attn_in,
        attn_out,
        gain_attn,
        gain_expert,
        router,
        expert_in[0],
        expert_out[0],
    )


def solution(mesh):
    return jax.shard_map(
        body,
        mesh=mesh,
        in_specs=(P(AXES, None), P(AXES, None), P(), P(), P(), P(), P(), P(AXES, None, None), P(AXES, None, None)),
        out_specs=P(AXES, None),
        check_vma=False,
    )
```
